512 devices in a mesh: sens: 4 (over z_lo), pts: 128 (over y, z_hi, x, core).
Axes of the slice: x: 4, y: 8, z: 8 (z_hi: 2, z_lo: 4; z = z_hi * 4 + z_lo), core: 2. Of those that a mesh axis runs over, the one named last changes fastest.
Arguments:
- params: float32 [24, 256, 2048], P('sens', 'pts'), may hold values from -6 to 6
- kernel: bfloat16 [2, 128, 2048, 257], P(None, 'sens', 'pts'), may hold values from -6 to 6
- coupled: int32 [128, 2048], P('sens', 'pts'), may hold values 0 or 1
- noise_prec: float32 [128, 256], P('sens'), may hold values from 4 to 32
- obs_len: int32 [128], P('sens'), may hold values from 128 to 256, as said below
Outputs:
- hessian_action: float32 [24, 256, 2048], P('sens', 'pts')
The draws below stay inside these ranges and needn't reach their ends.
Inputs may be any that keep to these rules, and one draw needn't show every extreme that they name: A sensor's record is live for the time steps t < obs_len; some sensor records all 256 steps and some only 128.
All inputs are finite; a program needn't handle non-finite values. No bound on the sum of `coupled` on one device may be relied on, other than what follows from the above.
Results may differ from the reference program's by a relative error of at most 0.0037.
Values may be sent and summed in bfloat16 or wider, within the bound.
A program may use at most 64 MiB of HBM per device.

```python
import math
import jax
import jax.numpy as jnp
from jax import lax

GY = 32
NS = 128
NP = 2048
NT = 256
NF = 257
R = 24
GX = 64


def draw_obs_len(key, part):
    drawn = jax.random.randint(jax.random.fold_in(key, 11), (NS,), NT // 2, NT + 1, dtype=jnp.int32)
    first = jax.random.randint(jax.random.fold_in(key, 12), (), 0, NS, dtype=jnp.int32)
    offset = jax.random.randint(jax.random.fold_in(key, 13), (), 1, NS, dtype=jnp.int32)
    second = (first + offset) % NS
    drawn = drawn.at[first].set(NT)
    return drawn.at[second].set(NT // 2)


def place_ends(entries, rng, smallest, high):
    shape = entries.shape
    place = [jax.random.randint(jax.random.fold_in(rng, axis), (), 0, shape[axis]) for axis in range(len(shape))]
    entries = entries.at[tuple(place)].set(smallest)
    longest = shape.index(max(shape))
    place[longest] = (place[longest] + 1) % shape[longest]
    return entries.at[tuple(place)].set(high)


def level_of(stream_key, shape, cuts, low, largest):
    level = 1.0
    for position, parts in cuts:
        draws = jax.random.uniform(jax.random.fold_in(jax.random.fold_in(stream_key, 6), position), (parts,), jnp.float32, low / len(cuts), largest / len(cuts))
        level = level * jnp.repeat(jnp.exp(draws), shape[position] // parts).reshape((-1,) + (1,) * (len(shape) - 1 - position))
    return level


def bell_draw(stream_key, extent, spread, limit, pieces=(), kind=jnp.bfloat16):
    entries = jax.random.normal(stream_key, extent, jnp.float32) * spread
    if len(pieces) > 0:
        entries = level_of(stream_key, extent, pieces, -0.22, 0.18) * entries
    return jnp.clip(entries, min=-limit, max=limit).astype(kind)


def setup_inputs(seed: int = 0) -> dict:
    key_of = jax.random.split(jax.random.key(seed), 6)
    params = bell_draw(key_of[0], (R, NT, NP), 1.0, 6.0, ((0, 4), (1, 128)), jnp.float32)
    kernel = bell_draw(key_of[1], (2, NS, NP, NF), 1.0, 6.0, ((1, 4), (2, 128)))
    coupled = place_ends((jax.random.randint(key_of[2], (NS, NP), 0, 4) < 3).astype(jnp.int32), jax.random.fold_in(key_of[2], 1), 0, 1)
    noise_prec = jnp.clip(jnp.exp(math.log(32.0) - 2.0794415 * jax.random.uniform(key_of[3], (NS, NT), jnp.float32) ** level_of(key_of[3], (NS, NT), ((0, 4),), -0.2, 0.2)), 4.0, 32.0)
    obs_len = draw_obs_len(jax.random.fold_in(key_of[5], 71), 0)
    return dict(params=params, kernel=kernel, coupled=coupled, noise_prec=noise_prec, obs_len=obs_len)


highest = lax.Precision.HIGHEST
prior_delta = 0.5
prior_gamma = 1.0

def dft_tables(steps):
    length = 2 * steps
    times = jnp.arange(steps, dtype=jnp.int32)
    freqs = jnp.arange(steps + 1, dtype=jnp.int32)
    phase = times[:, None] * freqs[None, :] % length
    angle = phase.astype(jnp.float32) * (2.0 * math.pi / length)
    factor = 1.0 / math.sqrt(length)
    cosine = jnp.cos(angle) * factor
    sine = jnp.sin(angle) * factor
    doubled = jnp.where((freqs == 0) | (freqs == steps), 1.0, 2.0).astype(jnp.float32)
    return (cosine, -sine, (cosine * doubled[None, :]).T, (-sine * doubled[None, :]).T)

def cosine_table(count):
    modes = jnp.arange(count, dtype=jnp.int32)
    cells = jnp.arange(count, dtype=jnp.int32)
    phase = modes[:, None] * (2 * cells[None, :] + 1) % (4 * count)
    angle = phase.astype(jnp.float32) * (math.pi / (2 * count))
    norms = jnp.where(modes == 0, math.sqrt(1.0 / count), math.sqrt(2.0 / count)).astype(jnp.float32)
    return jnp.cos(angle) * norms[:, None]

def prior_symbol(rows, cols):
    eigen_rows = 2.0 - 2.0 * jnp.cos(jnp.arange(rows, dtype=jnp.int32).astype(jnp.float32) * (math.pi / rows))
    eigen_cols = 2.0 - 2.0 * jnp.cos(jnp.arange(cols, dtype=jnp.int32).astype(jnp.float32) * (math.pi / cols))
    return 1.0 / (prior_delta + prior_gamma * (eigen_rows[:, None] + eigen_cols[None, :]))

def prior_filter(field, rows, cols):
    grid = field.reshape(field.shape[:-1] + (rows, cols))
    table_rows = cosine_table(rows)
    table_cols = cosine_table(cols)
    coeffs = jnp.einsum('ai,...ij->...aj', table_rows, grid, precision=highest)
    coeffs = jnp.einsum('...aj,bj->...ab', coeffs, table_cols, precision=highest)
    coeffs = coeffs * prior_symbol(rows, cols)
    back = jnp.einsum('...ab,bj->...aj', coeffs, table_cols, precision=highest)
    back = jnp.einsum('ai,...aj->...ij', table_rows, back, precision=highest)
    return back.reshape(field.shape)

def observe(freq_real, freq_imag, weight, tables):
    forward_cos, forward_sin, inverse_cos, inverse_sin = tables
    series = jnp.einsum('...f,ft->...t', freq_real, inverse_cos, precision=highest)
    series = series + jnp.einsum('...f,ft->...t', freq_imag, inverse_sin, precision=highest)
    series = series * weight
    real_part = jnp.einsum('...t,tf->...f', series, forward_cos, precision=highest)
    imag_part = jnp.einsum('...t,tf->...f', series, forward_sin, precision=highest)
    return jnp.stack([real_part, imag_part]).astype(jnp.bfloat16)

def reference(params, kernel, coupled, noise_prec, obs_len):
    tables = dft_tables(NT)
    forward_cos, forward_sin, inverse_cos, inverse_sin = tables
    filtered = prior_filter(params, GX, GY)
    spectra = jnp.stack([jnp.einsum('rtp,tf->prf', filtered, forward_cos, precision=highest), jnp.einsum('rtp,tf->prf', filtered, forward_sin, precision=highest)]).astype(jnp.bfloat16)
    masked = kernel * coupled[None, :, :, None].astype(jnp.bfloat16)
    kernel_real = masked[0].astype(jnp.float32)
    kernel_imag = masked[1].astype(jnp.float32)
    spectra_wide = spectra.astype(jnp.float32)
    with_real = jnp.einsum('spf,cprf->csrf', kernel_real, spectra_wide)
    with_imag = jnp.einsum('spf,cprf->csrf', kernel_imag, spectra_wide)
    observed = jnp.stack([with_real[0] - with_imag[1], with_real[1] + with_imag[0]]) * (1.0 / math.sqrt(NP))
    live = (jnp.arange(NT, dtype=jnp.int32)[None, :] < obs_len[:, None]).astype(jnp.float32)
    weight = (noise_prec * live)[:, None, :]
    residual = observe(observed[0], observed[1], weight, tables).astype(jnp.float32)
    back_real = jnp.einsum('spf,csrf->cprf', kernel_real, residual)
    back_imag = jnp.einsum('spf,csrf->cprf', kernel_imag, residual)
    adjoint = jnp.stack([back_real[0] + back_imag[1], back_real[1] - back_imag[0]]) * (1.0 / math.sqrt(NS))
    gradient = jnp.einsum('prf,ft->rtp', adjoint[0], inverse_cos, precision=highest)
    gradient = gradient + jnp.einsum('prf,ft->rtp', adjoint[1], inverse_sin, precision=highest)
    return prior_filter(gradient, GX, GY)
```

```python
import math

import jax
import jax.numpy as jnp
from jax import lax
from jax.sharding import PartitionSpec as P

GY = 32


highest = lax.Precision.HIGHEST
prior_delta = 0.5
prior_gamma = 1.0


def dft_tables(steps):
    length = 2 * steps
    times = jnp.arange(steps, dtype=jnp.int32)
    freqs = jnp.arange(steps + 1, dtype=jnp.int32)
    phase = times[:, None] * freqs[None, :] % length
    angle = phase.astype(jnp.float32) * (2.0 * math.pi / length)
    factor = 1.0 / math.sqrt(length)
    cosine = jnp.cos(angle) * factor
    sine = jnp.sin(angle) * factor
    doubled = jnp.where((freqs == 0) | (freqs == steps), 1.0, 2.0).astype(jnp.float32)
    return (cosine, -sine, (cosine * doubled[None, :]).T, (-sine * doubled[None, :]).T)


def cosine_table(count):
    modes = jnp.arange(count, dtype=jnp.int32)
    cells = jnp.arange(count, dtype=jnp.int32)
    phase = modes[:, None] * (2 * cells[None, :] + 1) % (4 * count)
    angle = phase.astype(jnp.float32) * (math.pi / (2 * count))
    norms = jnp.where(modes == 0, math.sqrt(1.0 / count), math.sqrt(2.0 / count)).astype(
        jnp.float32
    )
    return jnp.cos(angle) * norms[:, None]


def prior_symbol(rows, cols):
    eigen_rows = 2.0 - 2.0 * jnp.cos(
        jnp.arange(rows, dtype=jnp.int32).astype(jnp.float32) * (math.pi / rows)
    )
    eigen_cols = 2.0 - 2.0 * jnp.cos(
        jnp.arange(cols, dtype=jnp.int32).astype(jnp.float32) * (math.pi / cols)
    )
    return 1.0 / (prior_delta + prior_gamma * (eigen_rows[:, None] + eigen_cols[None, :]))


def prior_filter(field, rows, cols):
    grid = field.reshape(field.shape[:-1] + (rows, cols))
    table_rows = cosine_table(rows)
    table_cols = cosine_table(cols)
    coeffs = jnp.einsum("ai,...ij->...aj", table_rows, grid, precision=highest)
    coeffs = jnp.einsum("...aj,bj->...ab", coeffs, table_cols, precision=highest)
    coeffs = coeffs * prior_symbol(rows, cols)
    back = jnp.einsum("...ab,bj->...aj", coeffs, table_cols, precision=highest)
    back = jnp.einsum("ai,...aj->...ij", table_rows, back, precision=highest)
    return back.reshape(field.shape)


def transform(field, forward_cos, forward_sin):
    real_part = jnp.einsum("rtp,tf->prf", field, forward_cos, precision=highest)
    imag_part = jnp.einsum("rtp,tf->prf", field, forward_sin, precision=highest)
    return jnp.stack([real_part, imag_part]).astype(jnp.bfloat16)


def spread(values, axis):
    size = lax.axis_size(axis)
    copies = jnp.broadcast_to(values[None], (size,) + values.shape)
    return lax.all_to_all(copies, axis, split_axis=0, concat_axis=0, tiled=True)


def reduce_blocks(values, axis):
    pieces = lax.all_to_all(values, axis, split_axis=0, concat_axis=0, tiled=True)
    return jnp.sum(pieces, axis=0)


def on_device(params, kernel, coupled, noise_prec, obs_len):
    sens_rows = kernel.shape[1]
    points = kernel.shape[2]
    nfreq = kernel.shape[3]
    steps = nfreq - 1
    total_points = params.shape[2]
    grid_rows = total_points // GY
    sens_size = lax.axis_size("sens")
    pts_size = lax.axis_size("pts")
    own_rhs = params.shape[0]
    all_rhs = own_rhs * sens_size
    tables = dft_tables(steps)
    forward_cos, forward_sin, inverse_cos, inverse_sin = tables
    filtered = prior_filter(params, grid_rows, GY)
    points_field = lax.all_to_all(filtered, "pts", split_axis=2, concat_axis=1, tiled=True)
    own_spectra = transform(points_field, forward_cos, forward_sin)
    spectra = spread(own_spectra, "sens")
    spectra = spectra.transpose(1, 2, 0, 3, 4).reshape(2, points, all_rhs, nfreq)
    masked = kernel * coupled[None, :, :, None].astype(jnp.bfloat16)
    with_real = jnp.einsum("spf,cprf->csrf", masked[0], spectra, preferred_element_type=jnp.float32)
    with_imag = jnp.einsum("spf,cprf->csrf", masked[1], spectra, preferred_element_type=jnp.float32)
    series = jnp.einsum(
        "srf,ft->srt", with_real[0] - with_imag[1], inverse_cos, precision=highest
    )
    series = series + jnp.einsum(
        "srf,ft->srt", with_real[1] + with_imag[0], inverse_sin, precision=highest
    )
    rows = sens_rows * all_rhs // pts_size
    summed = reduce_blocks(series.reshape(pts_size, rows, steps), "pts")
    live = (jnp.arange(steps, dtype=jnp.int32)[None, :] < obs_len[:, None]).astype(jnp.float32)
    weight_rows = noise_prec * live
    row_ids = lax.axis_index("pts") * rows + jnp.arange(rows, dtype=jnp.int32)
    own_weight = weight_rows[row_ids // all_rhs]
    summed = summed * (own_weight * (1.0 / math.sqrt(total_points)))
    own_residual = jnp.stack(
        [
            jnp.einsum("gt,tf->gf", summed, forward_cos, precision=highest),
            jnp.einsum("gt,tf->gf", summed, forward_sin, precision=highest),
        ]
    ).astype(jnp.bfloat16)
    residual = spread(own_residual, "pts")
    residual = residual.transpose(1, 0, 2, 3).reshape(2, sens_rows, all_rhs, nfreq)
    back_real = jnp.einsum(
        "spf,csrf->cprf", masked[0], residual, preferred_element_type=jnp.float32
    )
    back_imag = jnp.einsum(
        "spf,csrf->cprf", masked[1], residual, preferred_element_type=jnp.float32
    )
    gradient = jnp.einsum(
        "prf,ft->rtp", back_real[0] + back_imag[1], inverse_cos, precision=highest
    )
    gradient = gradient + jnp.einsum(
        "prf,ft->rtp", back_real[1] - back_imag[0], inverse_sin, precision=highest
    )
    gradient = gradient.reshape(sens_size, own_rhs, steps, points)
    total_sensors = sens_rows * sens_size
    gradient = reduce_blocks(gradient, "sens") * (1.0 / math.sqrt(total_sensors))
    time_field = lax.all_to_all(gradient, "pts", split_axis=1, concat_axis=2, tiled=True)
    return prior_filter(time_field, grid_rows, GY)


def solution(mesh):
    placed = (
        P("sens", "pts", None),
        P(None, "sens", "pts", None),
        P("sens", "pts"),
        P("sens", None),
        P("sens"),
    )
    return jax.shard_map(
        on_device, mesh=mesh, in_specs=placed, out_specs=P("sens", "pts", None), check_vma=False
    )
```

```python
import math

import jax
import jax.numpy as jnp
import numpy as np
from jax import lax
from jax.experimental import pallas as pl
from jax.experimental.pallas import tpu as pltpu
from jax.sharding import PartitionSpec as P

GY = 32
HALF = GY // 2
LANES = 128
SUB = 8
prior_delta = 0.5
prior_gamma = 1.0
f32 = jnp.float32
bf16 = jnp.bfloat16
PTS_SHAPE = (8, 2, 4, 2)


def cosine_table(count):
    k = np.arange(count)[:, None]
    i = np.arange(count)[None, :]
    norm = np.where(k == 0, math.sqrt(1.0 / count), math.sqrt(2.0 / count))
    return np.cos(math.pi * k * (2 * i + 1) / (2 * count)) * norm


def prior_symbol(rows, cols):
    er = 2.0 - 2.0 * np.cos(math.pi * np.arange(rows) / rows)
    ec = 2.0 - 2.0 * np.cos(math.pi * np.arange(cols) / cols)
    return 1.0 / (prior_delta + prior_gamma * (er[:, None] + ec[None, :]))


def packed_dft(steps):
    t = np.arange(steps)[:, None]
    f = np.arange(steps)[None, :]
    angle = 2.0 * math.pi * ((t * f) % (2 * steps)) / (2 * steps)
    real, imag = np.cos(angle), -np.sin(angle)
    imag[:, 0] = np.cos(math.pi * t[:, 0])
    return np.concatenate([real, imag], axis=1) / math.sqrt(2 * steps)


def split_table(table):
    high = table.astype(np.float32).astype(bf16)
    low = (table - high.astype(np.float64)).astype(np.float32).astype(bf16)
    return np.stack([high, low])


def make_tables(grid_rows, shape, own_rhs, steps, lane_pad):
    ny, nz, nx, nc = shape
    nxc = nx * nc
    npts = ny * nz * nxc
    cx, cy = cosine_table(grid_rows), cosine_table(GY)
    fields = 2 * own_rhs
    per = LANES // GY
    cols_in = np.kron(np.eye(per), cy.T)
    cols_out = np.kron(np.eye(per), cy)
    spread_rows = np.repeat(cx.T, 2, axis=0)
    out_half = np.zeros((2, fields * GY, 2 * lane_pad))
    in_half = np.zeros((2, 2, lane_pad, fields * GY))
    for h in range(2):
        part = cy[:, h * HALF : (h + 1) * HALF]
        for r in range(own_rhs):
            for e in range(2):
                field = (2 * r + e) * GY
                lane = r * HALF
                out_half[h, field : field + GY, e * lane_pad + lane : e * lane_pad + lane + HALF] = part
                in_half[h, e, lane : lane + HALF, field : field + GY] = part.T
    row = np.arange(npts)
    xc, rest = row // (nz * ny), row % (nz * ny)
    z, y = rest // ny, rest % ny
    owner = (y * nz + z) * nxc + xc
    gather_rows = np.zeros((2 * grid_rows, npts))
    for h in range(2):
        gather_rows[h * grid_rows : (h + 1) * grid_rows] = cx[:, owner // 2] * (owner % 2 == h)[None, :]
    dft = packed_dft(steps)
    dft_pairs = np.stack([dft[2 * owner], dft[2 * owner + 1]])
    small = dict(cols_in=cols_in, cols_out=cols_out, cx=cx, cxt=cx.T, spread_rows=spread_rows)
    small.update(out_half=out_half, gather_rows=gather_rows, in_half=in_half, dft=dft, dft_pairs=dft_pairs)
    tables = {name: split_table(table) for name, table in small.items()}
    tables["sigma"] = np.tile(prior_symbol(grid_rows, GY), (1, per)).astype(np.float32)
    return tables


TABLES = ("cols_in", "cols_out", "cx", "cxt", "spread_rows", "out_half")
TABLES += ("gather_rows", "in_half", "dft", "dft_pairs", "sigma")

RIGHT = ((1,), (0,))
BOTH_LAST = ((1,), (1,))
BOTH_FIRST = ((0,), (0,))


def dot(a, b, dims):
    return lax.dot_general(a, b, (dims, ((), ())), preferred_element_type=f32)


def halves(v):
    high = v.astype(bf16)
    return high, (v - high.astype(f32)).astype(bf16)


def dot_table(v, high, low, dims=RIGHT):
    vh, vl = halves(v)
    return dot(vh, high, dims) + (dot(vl, high, dims) + dot(vh, low, dims))


def same_row(ref, j, s, p):
    return jnp.broadcast_to(ref[j, s, pl.ds(p, 1), :], (SUB, ref.shape[-1]))


def table_dot(high, low, v):
    vh, vl = halves(v)
    return dot(high, vh, RIGHT) + (dot(high, vl, RIGHT) + dot(low, vh, RIGHT))


def kernel_body(cfg, *refs):
    (ny, nz, nx, nc), ns = cfg["shape"], cfg["sens"]
    nxc, nyz = nx * nc, ny * nz
    npts = nyz * nxc
    sensors, points, steps, own_rhs = cfg["sensors"], cfg["points"], cfg["steps"], cfg["own_rhs"]
    rhs = own_rhs * ns
    lane_pad = cfg["lane_pad"]
    grid_rows = cfg["grid_rows"]
    tiles = sensors * rhs // SUB
    rtiles = rhs // SUB
    xt = tiles // (nc * nx)
    owners = cfg["owners"]
    yt = xt // owners
    chunks = 2 * own_rhs * GY // LANES
    rows = own_rhs * points
    per = LANES // GY
    width = min(LANES, steps)

    field_ref, kernel_hbm, mask_ref, noise_ref, len_ref = refs[:5]
    ntab = len(TABLES)
    table_hbm = refs[5 : 5 + ntab]
    out_ref = refs[5 + ntab]
    scratch = list(refs[6 + ntab :])
    table_vmem = scratch[:ntab]
    (kraw, k1, k2, k3, k4, s1, r1, r2, s3, r3, sp, xf, x1, x2, x3, obs, d0, rc, d1, rx, d2, ry, d3, rz) = scratch[
        ntab : ntab + 24
    ]
    (resb, q1, q2, q3, adj, gs, gk, rg, t1, u1, u2, s4, u3, flat, load_sem, send_sem, recv_sem) = scratch[ntab + 24 :]
    tab = dict(zip(TABLES, table_vmem))

    my_s = lax.axis_index("sens")
    me = lax.axis_index("pts")
    my_y = me // (nz * nxc)
    my_z = (me // nxc) % nz
    my_xc = me % nxc
    my_x = my_xc // nc
    my_c = my_xc % nc

    def pts_at(y, z, xc):
        return (y * nz + z) * nxc + xc

    loads = [pltpu.make_async_copy(a, b, load_sem.at[i]) for i, (a, b) in enumerate(zip(table_hbm, table_vmem))]
    loads.append(pltpu.make_async_copy(kernel_hbm, kraw, load_sem.at[ntab]))
    for copy in loads:
        copy.start()

    partners = [(my_s, pts_at((my_y + d) % ny, my_z, my_xc)) for d in range(1, ny)]
    partners += [(my_s, pts_at(my_y, (my_z + d) % nz, my_xc)) for d in range(1, nz)]
    partners += [(my_s, pts_at(my_y, my_z, (my_xc + d) % nxc)) for d in range(1, nxc)]
    partners += [((my_s + d) % ns, me) for d in range(1, ns)]
    barrier = pltpu.get_barrier_semaphore()
    for target in partners:
        pl.semaphore_signal(barrier, inc=1, device_id=target, device_id_type=pl.DeviceIdType.MESH)

    used = [0]

    spans = [pl.ds(j * width, width) for j in range(steps // width)]

    def push(src, dst, target):
        i = used[0]
        used[0] += 1
        return pltpu.make_async_remote_copy(
            src_ref=src,
            dst_ref=dst,
            send_sem=send_sem.at[i],
            recv_sem=recv_sem.at[i],
            device_id=target,
            device_id_type=pl.DeviceIdType.MESH,
        )

    def run(copies):
        for copy in copies:
            copy.start()
        return copies

    def finish(copies):
        for copy in copies:
            copy.wait()

    near_y = sorted(range(ny), key=lambda d: min(d, ny - d))

    def relay(copies, came, left):
        onward = []
        for d in near_y:
            y = (my_y + ny - d) % ny
            if d:
                copies[d - 1].wait_recv()
            for e in range(1, nz):
                z = (my_z + e) % nz
                onward += run([push(came.at[y, z], left.at[my_z, y], (my_s, pts_at(my_y, z, my_xc)))])
        left[my_z] = came[:, my_z]
        for copy in copies:
            copy.wait_send()
        finish(onward)

    def modes_out(z):
        return z * tab["sigma"][...]

    for copy in loads[:ntab]:
        copy.wait()
    parity = lax.broadcasted_iota(jnp.int32, (npts, 2 * lane_pad), 0) % 2
    filtered = [jnp.zeros((npts, 2 * lane_pad), f32)] * 2
    for g in range(chunks):
        z = jnp.zeros((grid_rows, LANES), f32)
        for i in range(per):
            lines = pl.ds(i * GY, GY)
            z = z + dot_table(field_ref[g * per + i], tab["cols_in"][0, lines, :], tab["cols_in"][1, lines, :])
        z = modes_out(table_dot(tab["cx"][0], tab["cx"][1], z))
        z = table_dot(tab["spread_rows"][0], tab["spread_rows"][1], z)
        for h in range(2):
            span = pl.ds(g * LANES, LANES)
            filtered[h] = filtered[h] + dot_table(z, tab["out_half"][0, h, span, :], tab["out_half"][1, h, span, :])
    mixed = jnp.where(parity == 0, filtered[0], filtered[1])
    for e in range(2):
        s1[:, :, e] = mixed[:, e * lane_pad : (e + 1) * lane_pad].reshape(ny, nz, nxc, lane_pad)

    pl.semaphore_wait(barrier, len(partners))
    copies = run(
        [
            push(s1.at[(my_y + d) % ny], r1.at[my_y], (my_s, pts_at((my_y + d) % ny, my_z, my_xc)))
            for d in range(1, ny)
        ]
    )
    r1[my_y] = s1[my_y]

    loads[ntab].wait()
    first16 = lax.broadcasted_iota(jnp.int32, (points, steps), 1) == 0

    for s in range(sensors):
        keep = mask_ref[:, s : s + 1].astype(f32)
        real = kraw[0, s, :, :steps].astype(f32)
        imag = kraw[1, s, :, :steps].astype(f32)
        last = kraw[0, s, :, steps : steps + 1].astype(f32)
        imag = jnp.where(first16, 0.0, imag)
        plain = jnp.where(first16, last, real)
        for ref, value in ((k1, real + imag), (k2, plain), (k3, imag), (k4, real - imag)):
            for j, span in enumerate(spans):
                ref[j, s] = (value * keep)[:, j * width : (j + 1) * width]

    relay(copies, r1, r2)
    flat[...] = r2[...].reshape(nyz * 2 * nxc, lane_pad)
    for j in range(nxc):
        for e in range(2):
            s3[j, e] = flat[pl.ds(e * nxc + j, nyz, stride=2 * nxc), :]
    copies = run(
        [
            push(s3.at[(my_xc + d) % nxc], r3.at[my_xc], (my_s, pts_at(my_y, my_z, (my_xc + d) % nxc)))
            for d in range(1, nxc)
        ]
    )
    r3[my_xc] = s3[my_xc]
    finish(copies)

    spectra = jnp.zeros((lane_pad, 2 * steps), f32)
    for e in range(2):
        series = r3[:, e].reshape(npts, lane_pad)
        spectra = spectra + dot_table(series, tab["dft_pairs"][0, e], tab["dft_pairs"][1, e], BOTH_FIRST)
    sp[my_s] = spectra[:rows].astype(bf16)
    finish(run([push(sp.at[my_s], sp.at[my_s], ((my_s + d) % ns, me)) for d in range(1, ns)]))
    for k in range(ns):
        for q in range(2 * steps // width):
            xf[q, k * rows : (k + 1) * rows] = sp[k, :, q * width : (q + 1) * width].astype(f32)
    first_r = lax.broadcasted_iota(jnp.int32, (rhs, width), 1) == 0
    first_8 = lax.broadcasted_iota(jnp.int32, (SUB, width), 1) == 0
    for p in range(points):
        for j, span in enumerate(spans):
            c = xf[j, pl.ds(p, rhs, stride=points), :]
            d = xf[len(spans) + j, pl.ds(p, rhs, stride=points), :]
            x1[p, :, span] = c
            x2[p, :, span] = jnp.where(first_r, d, d - c) if j == 0 else d - c
            x3[p, :, span] = c + d

    def combine(real_terms, j, out, at):
        p1, p2, real = real_terms
        imag = p1 + p2
        if j == 0:
            out[at + (pl.ds(0, width),)] = jnp.where(first_8, real, real + real)
            out[at + (pl.ds(steps, width),)] = jnp.where(first_8, p2, imag + imag)
        else:
            out[at + (spans[j],)] = real + real
            out[at + (pl.ds(steps + j * width, width),)] = imag + imag

    def contract(i, carry):
        for j, span in enumerate(spans):
            acc = {}
            for p in range(points):
                for u in range(2):
                    ka, kb, kc = (same_row(k, j, 2 * i + u, p) for k in (k1, k2, k3))
                    for b in range(rtiles):
                        rr = pl.ds(b * SUB, SUB)
                        term = (ka * x1[p, rr, span], kb * x2[p, rr, span], kc * x3[p, rr, span])
                        old = acc.get((u, b))
                        acc[u, b] = term if old is None else tuple(o + t for o, t in zip(old, term))
            for (u, b), (p1, p2, p3) in acc.items():
                combine((p1, p2, p1 - p3), j, obs, (2 * i + u, pl.ds(b * SUB, SUB)))
        return carry

    block = xt // rtiles

    def predict(c, x):
        first = (c * nx + x) * block
        lax.fori_loop(first // 2, (first + block) // 2, contract, 0)
        value = obs[pl.ds(first, block)].reshape(block * rhs, 2 * steps)
        value = dot_table(value, tab["dft"][0], tab["dft"][1], BOTH_LAST)
        d0[c * nx + x] = value.reshape(xt, SUB, steps)

    other_c = (my_c + 1) % nc
    other = pts_at(my_y, my_z, my_x * nc + other_c)
    base_c, base_x = used[0], used[0] + nx
    used[0] += 2 * nx

    def place(i):
        return (my_x + i + 1) % nx

    def core_copy(i):
        x = place(i)
        return pltpu.make_async_remote_copy(
            src_ref=d0.at[other_c * nx + x],
            dst_ref=rc.at[x],
            send_sem=send_sem.at[base_c + i],
            recv_sem=recv_sem.at[base_c + i],
            device_id=(my_s, other),
            device_id_type=pl.DeviceIdType.MESH,
        )

    def x_copy(i):
        x = place(i)
        return pltpu.make_async_remote_copy(
            src_ref=d1.at[x],
            dst_ref=rx.at[i],
            send_sem=send_sem.at[base_x + i],
            recv_sem=recv_sem.at[base_x + i],
            device_id=(my_s, pts_at(my_y, my_z, x * nc + my_c)),
            device_id_type=pl.DeviceIdType.MESH,
        )

    def arrived(i):
        x = place(i)
        core_copy(i).wait_recv()
        d1[x] = d0[my_c * nx + x] + rc[x]

    def step(i, carry):
        predict(other_c, place(i))
        core_copy(i).start()
        predict(my_c, place(i))

        @pl.when(i > 0)
        def _():
            arrived(i - 1)
            x_copy(i - 1).start()

        return carry

    lax.fori_loop(0, nx, step, 0)
    arrived(nx - 1)
    total = d1[my_x]
    for i in range(nx - 1):
        x_copy(i).wait()
        total = total + rx[i]
    d2[...] = total
    for i in range(nx):
        core_copy(i).wait_send()

    owning = my_y < owners
    copies = [
        push(
            d2.at[pl.ds(lax.rem((my_y + d) % ny, owners) * yt, yt)],
            ry.at[d - 1],
            (my_s, pts_at((my_y + d) % ny, my_z, my_xc)),
        )
        for d in range(1, ny)
    ]
    for d, copy in zip(range(1, ny), copies):
        pl.when((my_y + d) % ny < owners)(copy.start)
    for d, copy in zip(range(1, ny), copies):
        pl.when((my_y + d) % ny < owners)(copy.wait_send)
        pl.when(owning)(copy.wait_recv)

    first_tile = (my_c * nx + my_x) * xt
    held = lax.rem(my_y, owners)
    y_tile = first_tile + held * yt
    z_copies = [push(d3, rz.at[my_z], (my_s, pts_at(my_y, (my_z + d) % nz, my_xc))) for d in range(1, nz)]

    @pl.when(owning)
    def _():
        total = d2[pl.ds(held * yt, yt)]
        for d in range(1, ny):
            total = total + ry[d - 1]
        d3[...] = total
        finish(run(z_copies))
        rz[my_z] = d3[...]
        total = rz[0]
        for z in range(1, nz):
            total = total + rz[z]
        for i in range(yt):
            s = (y_tile + i) // rtiles
            live = lax.broadcasted_iota(jnp.int32, (1, steps), 1) < len_ref[s]
            weight = jnp.where(live, noise_ref[pl.ds(s, 1), :], 0.0) * cfg["scale_points"]
            value = dot_table(total[i] * weight, tab["dft"][0], tab["dft"][1])
            resb[y_tile + i] = value.astype(bf16)

    def piece(c, x, y):
        return resb.at[pl.ds((c * nx + x) * xt + lax.rem(y, owners) * yt, yt)]

    mine = piece(my_c, my_x, my_y)
    y_copies = [push(mine, mine, (my_s, pts_at((my_y + d) % ny, my_z, my_xc))) for d in range(1, ny)]
    for copy in y_copies:
        pl.when(owning)(copy.start)
    x_copies, c_copies = {}, {}
    for d in near_y:
        y = (my_y + ny - d) % ny
        if d:
            pl.when(y < owners)(y_copies[d - 1].wait_recv)
        here = piece(my_c, my_x, y)
        x_copies[d] = [
            push(here, here, (my_s, pts_at(my_y, my_z, ((my_x + e) % nx) * nc + my_c))) for e in range(1, nx)
        ]
        sources = [piece(my_c, (my_x + nx - e) % nx, y) for e in range(nx)]
        c_copies[d] = [push(source, source, (my_s, other)) for source in sources]
        pl.when(y < owners)(lambda d=d: run(x_copies[d] + c_copies[d][:1]) and None)
    for d in near_y:
        y = (my_y + ny - d) % ny

        @pl.when(y < owners)
        def _(d=d):
            for e in range(1, nx):
                x_copies[d][e - 1].wait_recv()
                c_copies[d][e].start()

    for copy in y_copies:
        pl.when(owning)(copy.wait_send)
    for d in near_y:
        y = (my_y + ny - d) % ny

        @pl.when(y < owners)
        def _(d=d):
            for copy in x_copies[d]:
                copy.wait_send()
            finish(c_copies[d])

    def widen(s, carry):
        for b in range(rtiles):
            rr = pl.ds(b * SUB, SUB)
            for j, span in enumerate(spans):
                c = resb[s * rtiles + b, :, span].astype(f32)
                d = resb[s * rtiles + b, :, pl.ds(steps + j * width, width)].astype(f32)
                q1[s, rr, span] = c
                q2[s, rr, span] = jnp.where(first_8, d, d - c) if j == 0 else d - c
                q3[s, rr, span] = c + d
        return carry

    lax.fori_loop(0, sensors, widen, 0)

    def contract_back(i, carry):
        for j, span in enumerate(spans):
            acc = {}
            for s in range(sensors):
                for u in range(2):
                    ka, kb, kc = (same_row(k, j, s, 2 * i + u) for k in (k4, k2, k3))
                    for b in range(rtiles):
                        rr = pl.ds(b * SUB, SUB)
                        term = (ka * q1[s, rr, span], kb * q2[s, rr, span], kc * q3[s, rr, span])
                        old = acc.get((u, b))
                        acc[u, b] = term if old is None else tuple(o + t for o, t in zip(old, term))
            for (u, b), (p1, p2, p3) in acc.items():
                combine((p1, p2, p1 + p3), j, adj, (2 * i + u, pl.ds(b * SUB, SUB)))
        return carry

    lax.fori_loop(0, points // 2, contract_back, 0)

    value = dot_table(adj[...].reshape(points * rhs, 2 * steps), tab["dft"][0], tab["dft"][1], BOTH_LAST)
    for j in range(len(spans)):
        gs[j] = value[:, j * width : (j + 1) * width]
    for r in range(rhs):
        for j, span in enumerate(spans):
            gk[r // own_rhs, pl.ds((r % own_rhs) * points, points), span] = gs[
                j, pl.ds(r, points, stride=rhs), :
            ].astype(bf16)

    finish(run([push(gk.at[(my_s + d) % ns], rg.at[d - 1], ((my_s + d) % ns, me)) for d in range(1, ns)]))
    total = gk[my_s].astype(f32)
    for d in range(1, ns):
        total = total + rg[d - 1].astype(f32)
    total = total * cfg["scale_sensors"]
    if rows < lane_pad:
        total = jnp.concatenate([total, jnp.zeros((lane_pad - rows, steps), f32)], axis=0)
    t1[...] = jnp.transpose(total).reshape(ny, nz, 2 * nxc, lane_pad)

    copies = run(
        [
            push(t1.at[(my_y + d) % ny], u1.at[my_y], (my_s, pts_at((my_y + d) % ny, my_z, my_xc)))
            for d in range(1, ny)
        ]
    )
    u1[my_y] = t1[my_y]
    relay(copies, u1, u2)
    flat[...] = u2[...].reshape(nyz * 2 * nxc, lane_pad)
    for j in range(nxc):
        for e in range(2):
            s4[j, e] = flat[pl.ds(2 * j + e, nyz, stride=2 * nxc), :]
    copies = run(
        [
            push(s4.at[(my_xc + d) % nxc], u3.at[my_xc], (my_s, pts_at(my_y, my_z, (my_xc + d) % nxc)))
            for d in range(1, nxc)
        ]
    )
    u3[my_xc] = s4[my_xc]
    finish(copies)

    modes = jnp.zeros((grid_rows, chunks * LANES), f32)
    for e in range(2):
        field = u3[:, e].reshape(npts, lane_pad)
        field = table_dot(tab["gather_rows"][0], tab["gather_rows"][1], field)
        for h in range(2):
            part = field[h * grid_rows : (h + 1) * grid_rows]
            modes = modes + dot_table(part, tab["in_half"][0, h, e], tab["in_half"][1, h, e])
    for g in range(chunks):
        z = modes_out(modes[:, g * LANES : (g + 1) * LANES])
        z = table_dot(tab["cxt"][0], tab["cxt"][1], z)
        z = dot_table(z, tab["cols_out"][0], tab["cols_out"][1])
        for i in range(per):
            out_ref[g * per + i] = z[:, i * GY : (i + 1) * GY]


def on_device(shape, params, kernel, coupled, noise_prec, obs_len):
    ny, nz, nx, nc = shape
    ns = lax.axis_size("sens")
    npts = lax.axis_size("pts")
    own_rhs, own_steps, total_points = params.shape
    sensors, points, steps = kernel.shape[1], kernel.shape[2], kernel.shape[3] - 1
    grid_rows = total_points // GY
    rhs = own_rhs * ns
    lane_pad = LANES
    tiles = sensors * rhs // SUB
    xt = tiles // (nc * nx)
    owners = max(k for k in range(1, ny + 1) if xt % k == 0)
    yt = xt // owners
    rows = own_rhs * points
    fields = own_rhs * own_steps
    assert xt % (2 * (rhs // SUB)) == 0
    assert own_steps == 2 and points == HALF and npts == ny * nz * nx * nc and rows <= lane_pad
    cfg = dict(
        shape=shape,
        sens=ns,
        sensors=sensors,
        points=points,
        steps=steps,
        own_rhs=own_rhs,
        lane_pad=lane_pad,
        grid_rows=grid_rows,
        owners=owners,
        scale_points=1.0 / math.sqrt(total_points),
        scale_sensors=1.0 / math.sqrt(sensors * ns),
    )
    tables = make_tables(grid_rows, shape, own_rhs, steps, lane_pad)
    tables = [jnp.asarray(tables[name]) for name in TABLES]
    field = params.reshape(fields, grid_rows, GY)
    nxc, nyz = nx * nc, ny * nz
    vm = pltpu.VMEM
    scratch = [vm(t.shape, t.dtype) for t in tables]
    scratch += [vm(kernel.shape, kernel.dtype)]
    scratch += [vm((steps // min(LANES, steps), sensors, points, min(LANES, steps)), f32)] * 4
    scratch += [vm((ny, nz, 2, nxc, lane_pad), f32)] * 2
    scratch += [vm((nz, ny, 2, nxc, lane_pad), f32)]
    scratch += [vm((nxc, 2, nyz, lane_pad), f32)] * 2
    scratch += [vm((ns, rows, 2 * steps), bf16), vm((2 * steps // min(LANES, steps), ns * rows, min(LANES, steps)), f32)]
    scratch += [vm((points, rhs, steps), f32)] * 3
    scratch += [vm((sensors, rhs, 2 * steps), f32)]
    scratch += [vm((nc * nx, xt, SUB, steps), f32)] + [vm((nx, xt, SUB, steps), f32)] * 2
    scratch += [vm((max(nx - 1, 1), xt, SUB, steps), f32), vm((xt, SUB, steps), f32)]
    scratch += [vm((max(ny - 1, 1), yt, SUB, steps), f32), vm((yt, SUB, steps), f32)]
    scratch += [vm((nz, yt, SUB, steps), f32)]
    scratch += [vm((tiles, SUB, 2 * steps), bf16)]
    scratch += [vm((sensors, rhs, steps), f32)] * 3
    scratch += [vm((points, rhs, 2 * steps), f32), vm((steps // min(LANES, steps), points * rhs, min(LANES, steps)), f32)]
    scratch += [vm((ns, rows, steps), bf16), vm((max(ns - 1, 1), rows, steps), bf16)]
    scratch += [vm((ny, nz, 2 * nxc, lane_pad), f32)] * 2 + [vm((nz, ny, 2 * nxc, lane_pad), f32)]
    scratch += [vm((nxc, 2, nyz, lane_pad), f32)] * 2
    scratch += [vm((nyz * 2 * nxc, lane_pad), f32)]
    copies = 4 * ny + 2 * ny * nz + 2 * nxc + 2 * ns + 4 * nx + 2 * ny * nx + nz
    scratch += [
        pltpu.SemaphoreType.DMA((len(tables) + 1,)),
        pltpu.SemaphoreType.DMA((copies,)),
        pltpu.SemaphoreType.DMA((copies,)),
    ]
    whole = pl.BlockSpec(memory_space=pltpu.VMEM)
    scalars = pl.BlockSpec(memory_space=pltpu.SMEM)
    anywhere = pl.BlockSpec(memory_space=pl.ANY)
    out = pl.pallas_call(
        lambda *refs: kernel_body(cfg, *refs),
        out_shape=jax.ShapeDtypeStruct((fields, grid_rows, GY), f32),
        in_specs=[whole, anywhere, whole, whole, scalars] + [anywhere] * len(tables),
        out_specs=whole,
        scratch_shapes=scratch,
        compiler_params=pltpu.CompilerParams(
            collective_id=0, has_side_effects=True, vmem_limit_bytes=60 * 1024 * 1024
        ),
        name="hessian_action",
    )(field, kernel, coupled.T, noise_prec, obs_len, *tables)
    return out.reshape(params.shape)


def solution(mesh, shape=PTS_SHAPE):
    placed = (
        P("sens", "pts", None),
        P(None, "sens", "pts", None),
        P("sens", "pts"),
        P("sens", None),
        P("sens"),
    )
    return jax.shard_map(
        lambda *args: on_device(shape, *args),
        mesh=mesh,
        in_specs=placed,
        out_specs=P("sens", "pts", None),
        check_vma=False,
    )
```

```python
import math

import jax
import jax.numpy as jnp
import numpy as np
from jax import lax
from jax.experimental import pallas as pl
from jax.experimental.pallas import tpu as pltpu
from jax.sharding import PartitionSpec as P

GY = 32
HALF = GY // 2
LANES = 128
SUB = 8
prior_delta = 0.5
prior_gamma = 1.0
f32 = jnp.float32
bf16 = jnp.bfloat16
PTS_SHAPE = (8, 2, 4, 2)


def cosine_table(count):
    k = np.arange(count)[:, None]
    i = np.arange(count)[None, :]
    norm = np.where(k == 0, math.sqrt(1.0 / count), math.sqrt(2.0 / count))
    return np.cos(math.pi * k * (2 * i + 1) / (2 * count)) * norm


def prior_symbol(rows, cols):
    er = 2.0 - 2.0 * np.cos(math.pi * np.arange(rows) / rows)
    ec = 2.0 - 2.0 * np.cos(math.pi * np.arange(cols) / cols)
    return 1.0 / (prior_delta + prior_gamma * (er[:, None] + ec[None, :]))


def packed_dft(steps):
    t = np.arange(steps)[:, None]
    f = np.arange(steps)[None, :]
    angle = 2.0 * math.pi * ((t * f) % (2 * steps)) / (2 * steps)
    real, imag = np.cos(angle), -np.sin(angle)
    imag[:, 0] = np.cos(math.pi * t[:, 0])
    return np.concatenate([real, imag], axis=1) / math.sqrt(2 * steps)


def split_table(table):
    high = table.astype(np.float32).astype(bf16)
    low = (table - high.astype(np.float64)).astype(np.float32).astype(bf16)
    return np.stack([high, low])


def make_tables(grid_rows, shape, own_rhs, steps, lane_pad):
    ny, nz, nx, nc = shape
    nxc = nx * nc
    npts = ny * nz * nxc
    cx, cy = cosine_table(grid_rows), cosine_table(GY)
    fields = 2 * own_rhs
    per = LANES // GY
    cols_in = np.kron(np.eye(per), cy.T)
    cols_out = np.kron(np.eye(per), cy)
    spread_rows = np.repeat(cx.T, 2, axis=0)
    out_half = np.zeros((2, fields * GY, 2 * lane_pad))
    in_half = np.zeros((2, 2, lane_pad, fields * GY))
    for h in range(2):
        part = cy[:, h * HALF : (h + 1) * HALF]
        for r in range(own_rhs):
            for e in range(2):
                field = (2 * r + e) * GY
                lane = r * HALF
                out_half[h, field : field + GY, e * lane_pad + lane : e * lane_pad + lane + HALF] = part
                in_half[h, e, lane : lane + HALF, field : field + GY] = part.T
    row = np.arange(npts)
    xc, rest = row // (nz * ny), row % (nz * ny)
    z, y = rest // ny, rest % ny
    owner = (y * nz + z) * nxc + xc
    gather_rows = np.zeros((2 * grid_rows, npts))
    for h in range(2):
        gather_rows[h * grid_rows : (h + 1) * grid_rows] = cx[:, owner // 2] * (owner % 2 == h)[None, :]
    dft = packed_dft(steps)
    dft_pairs = np.stack([dft[2 * owner], dft[2 * owner + 1]])
    small = dict(cols_in=cols_in, cols_out=cols_out, cx=cx, cxt=cx.T, spread_rows=spread_rows)
    small.update(out_half=out_half, gather_rows=gather_rows, in_half=in_half, dft=dft, dft_pairs=dft_pairs)
    tables = {name: split_table(table) for name, table in small.items()}
    tables["sigma"] = np.tile(prior_symbol(grid_rows, GY), (1, per)).astype(np.float32)
    return tables


TABLES = ("cols_in", "cx", "sigma", "spread_rows", "out_half")
FIRST = len(TABLES)
TABLES += ("dft_pairs", "dft", "gather_rows", "in_half")
TABLES += ("cols_out", "cxt")

RIGHT = ((1,), (0,))
BOTH_LAST = ((1,), (1,))
BOTH_FIRST = ((0,), (0,))


def dot(a, b, dims):
    return lax.dot_general(a, b, (dims, ((), ())), preferred_element_type=f32)


def halves(v):
    high = v.astype(bf16)
    return high, (v - high.astype(f32)).astype(bf16)


def dot_table(v, high, low, dims=RIGHT):
    vh, vl = halves(v)
    return dot(vh, high, dims) + (dot(vl, high, dims) + dot(vh, low, dims))


def same_row(ref, j, s, p):
    return jnp.broadcast_to(ref[j, s, pl.ds(p, 1), :], (SUB, ref.shape[-1]))


def table_dot(high, low, v):
    vh, vl = halves(v)
    return dot(high, vh, RIGHT) + (dot(high, vl, RIGHT) + dot(low, vh, RIGHT))


def kernel_body(cfg, *refs):
    (ny, nz, nx, nc), ns = cfg["shape"], cfg["sens"]
    nxc, nyz = nx * nc, ny * nz
    npts = nyz * nxc
    sensors, points, steps, own_rhs = cfg["sensors"], cfg["points"], cfg["steps"], cfg["own_rhs"]
    rhs = own_rhs * ns
    lane_pad = cfg["lane_pad"]
    grid_rows = cfg["grid_rows"]
    tiles = sensors * rhs // SUB
    rtiles = rhs // SUB
    xt = tiles // (nc * nx)
    owners = cfg["owners"]
    yt = xt // owners
    chunks = 2 * own_rhs * GY // LANES
    rows = own_rhs * points
    per = LANES // GY
    width = min(LANES, steps)

    field_ref, kernel_hbm, mask_ref, noise_ref, len_ref = refs[:5]
    ntab = len(TABLES)
    table_hbm = refs[5 : 5 + ntab]
    out_ref = refs[5 + ntab]
    scratch = list(refs[6 + ntab :])
    table_vmem = scratch[:ntab]
    (kraw, k1, k2, k3, k4, s1, r1, r2, s3, r3, sp, xf, x1, x2, x3, obs, d0, rc, d1, rx, d2, ry, d3, rz) = scratch[
        ntab : ntab + 24
    ]
    (resb, q1, q2, q3, adj, gs, gk, rg, t1, u1, u2, s4, u3, flat, load_sem, send_sem, recv_sem) = scratch[ntab + 24 :]
    tab = dict(zip(TABLES, table_vmem))

    my_s = lax.axis_index("sens")
    me = lax.axis_index("pts")
    my_y = me // (nz * nxc)
    my_z = (me // nxc) % nz
    my_xc = me % nxc
    my_x = my_xc // nc
    my_c = my_xc % nc

    def pts_at(y, z, xc):
        return (y * nz + z) * nxc + xc

    loads = [pltpu.make_async_copy(a, b, load_sem.at[i]) for i, (a, b) in enumerate(zip(table_hbm, table_vmem))]
    loads.append(pltpu.make_async_copy(kernel_hbm, kraw, load_sem.at[ntab]))
    for copy in loads:
        copy.start()

    partners = [(my_s, pts_at((my_y + d) % ny, my_z, my_xc)) for d in range(1, ny)]
    partners += [(my_s, pts_at(my_y, (my_z + d) % nz, my_xc)) for d in range(1, nz)]
    partners += [(my_s, pts_at(my_y, my_z, (my_xc + d) % nxc)) for d in range(1, nxc)]
    partners += [((my_s + d) % ns, me) for d in range(1, ns)]
    barrier = pltpu.get_barrier_semaphore()
    for target in partners:
        pl.semaphore_signal(barrier, inc=1, device_id=target, device_id_type=pl.DeviceIdType.MESH)

    used = [0]

    spans = [pl.ds(j * width, width) for j in range(steps // width)]

    def push(src, dst, target):
        i = used[0]
        used[0] += 1
        return pltpu.make_async_remote_copy(
            src_ref=src,
            dst_ref=dst,
            send_sem=send_sem.at[i],
            recv_sem=recv_sem.at[i],
            device_id=target,
            device_id_type=pl.DeviceIdType.MESH,
        )

    def run(copies):
        for copy in copies:
            copy.start()
        return copies

    def finish(copies):
        for copy in copies:
            copy.wait()

    near_y = sorted(range(ny), key=lambda d: min(d, ny - d))

    def relay(copies, came, left):
        onward = []
        for d in near_y:
            y = (my_y + ny - d) % ny
            if d:
                copies[d - 1].wait_recv()
            for e in range(1, nz):
                z = (my_z + e) % nz
                onward += run([push(came.at[y, z], left.at[my_z, y], (my_s, pts_at(my_y, z, my_xc)))])
        left[my_z] = came[:, my_z]
        for copy in copies:
            copy.wait_send()
        finish(onward)

    def modes_out(z):
        return z * tab["sigma"][...]

    for copy in loads[:FIRST]:
        copy.wait()
    parity = lax.broadcasted_iota(jnp.int32, (npts, 2 * lane_pad), 0) % 2
    filtered = [jnp.zeros((npts, 2 * lane_pad), f32)] * 2
    for g in range(chunks):
        z = jnp.zeros((grid_rows, LANES), f32)
        for i in range(per):
            lines = pl.ds(i * GY, GY)
            z = z + dot_table(field_ref[g * per + i], tab["cols_in"][0, lines, :], tab["cols_in"][1, lines, :])
        z = modes_out(table_dot(tab["cx"][0], tab["cx"][1], z))
        z = table_dot(tab["spread_rows"][0], tab["spread_rows"][1], z)
        for h in range(2):
            span = pl.ds(g * LANES, LANES)
            filtered[h] = filtered[h] + dot_table(z, tab["out_half"][0, h, span, :], tab["out_half"][1, h, span, :])
    mixed = jnp.where(parity == 0, filtered[0], filtered[1])
    for e in range(2):
        s1[:, :, e] = mixed[:, e * lane_pad : (e + 1) * lane_pad].reshape(ny, nz, nxc, lane_pad)

    pl.semaphore_wait(barrier, len(partners))
    copies = run(
        [
            push(s1.at[(my_y + d) % ny], r1.at[my_y], (my_s, pts_at((my_y + d) % ny, my_z, my_xc)))
            for d in range(1, ny)
        ]
    )
    r1[my_y] = s1[my_y]

    for copy in loads[FIRST:]:
        copy.wait()
    first16 = lax.broadcasted_iota(jnp.int32, (points, steps), 1) == 0

    for s in range(sensors):
        keep = mask_ref[:, s : s + 1].astype(f32)
        real = kraw[0, s, :, :steps].astype(f32)
        imag = kraw[1, s, :, :steps].astype(f32)
        last = kraw[0, s, :, steps : steps + 1].astype(f32)
        imag = jnp.where(first16, 0.0, imag)
        plain = jnp.where(first16, last, real)
        for ref, value in ((k1, real + imag), (k2, plain), (k3, imag), (k4, real - imag)):
            for j, span in enumerate(spans):
                ref[j, s] = (value * keep)[:, j * width : (j + 1) * width]

    relay(copies, r1, r2)
    flat[...] = r2[...].reshape(nyz * 2 * nxc, lane_pad)
    for j in range(nxc):
        for e in range(2):
            s3[j, e] = flat[pl.ds(e * nxc + j, nyz, stride=2 * nxc), :]
    copies = run(
        [
            push(s3.at[(my_xc + d) % nxc], r3.at[my_xc], (my_s, pts_at(my_y, my_z, (my_xc + d) % nxc)))
            for d in range(1, nxc)
        ]
    )
    r3[my_xc] = s3[my_xc]
    finish(copies)

    spectra = jnp.zeros((lane_pad, 2 * steps), f32)
    for e in range(2):
        series = r3[:, e].reshape(npts, lane_pad)
        spectra = spectra + dot_table(series, tab["dft_pairs"][0, e], tab["dft_pairs"][1, e], BOTH_FIRST)
    sp[my_s] = spectra[:rows].astype(bf16)
    finish(run([push(sp.at[my_s], sp.at[my_s], ((my_s + d) % ns, me)) for d in range(1, ns)]))
    for k in range(ns):
        for q in range(2 * steps // width):
            xf[q, k * rows : (k + 1) * rows] = sp[k, :, q * width : (q + 1) * width].astype(f32)
    first_r = lax.broadcasted_iota(jnp.int32, (rhs, width), 1) == 0
    first_8 = lax.broadcasted_iota(jnp.int32, (SUB, width), 1) == 0
    for p in range(points):
        for j, span in enumerate(spans):
            c = xf[j, pl.ds(p, rhs, stride=points), :]
            d = xf[len(spans) + j, pl.ds(p, rhs, stride=points), :]
            x1[p, :, span] = c
            x2[p, :, span] = jnp.where(first_r, d, d - c) if j == 0 else d - c
            x3[p, :, span] = c + d

    def combine(real_terms, j, out, at):
        p1, p2, real = real_terms
        imag = p1 + p2
        if j == 0:
            out[at + (pl.ds(0, width),)] = jnp.where(first_8, real, real + real)
            out[at + (pl.ds(steps, width),)] = jnp.where(first_8, p2, imag + imag)
        else:
            out[at + (spans[j],)] = real + real
            out[at + (pl.ds(steps + j * width, width),)] = imag + imag

    def contract(i, carry):
        for j, span in enumerate(spans):
            acc = {}
            for p in range(points):
                for u in range(2):
                    ka, kb, kc = (same_row(k, j, 2 * i + u, p) for k in (k1, k2, k3))
                    for b in range(rtiles):
                        rr = pl.ds(b * SUB, SUB)
                        term = (ka * x1[p, rr, span], kb * x2[p, rr, span], kc * x3[p, rr, span])
                        old = acc.get((u, b))
                        acc[u, b] = term if old is None else tuple(o + t for o, t in zip(old, term))
            for (u, b), (p1, p2, p3) in acc.items():
                combine((p1, p2, p1 - p3), j, obs, (2 * i + u, pl.ds(b * SUB, SUB)))
        return carry

    block = xt // rtiles

    def predict(c, x):
        first = (c * nx + x) * block
        lax.fori_loop(first // 2, (first + block) // 2, contract, 0)
        value = obs[pl.ds(first, block)].reshape(block * rhs, 2 * steps)
        value = dot_table(value, tab["dft"][0], tab["dft"][1], BOTH_LAST)
        d0[c * nx + x] = value.reshape(xt, SUB, steps)

    other_c = (my_c + 1) % nc
    other = pts_at(my_y, my_z, my_x * nc + other_c)
    base_c, base_x = used[0], used[0] + nx
    used[0] += 2 * nx

    def place(i):
        return (my_x + i + 1) % nx

    def core_copy(i):
        x = place(i)
        return pltpu.make_async_remote_copy(
            src_ref=d0.at[other_c * nx + x],
            dst_ref=rc.at[x],
            send_sem=send_sem.at[base_c + i],
            recv_sem=recv_sem.at[base_c + i],
            device_id=(my_s, other),
            device_id_type=pl.DeviceIdType.MESH,
        )

    def x_copy(i):
        x = place(i)
        return pltpu.make_async_remote_copy(
            src_ref=d1.at[x],
            dst_ref=rx.at[i],
            send_sem=send_sem.at[base_x + i],
            recv_sem=recv_sem.at[base_x + i],
            device_id=(my_s, pts_at(my_y, my_z, x * nc + my_c)),
            device_id_type=pl.DeviceIdType.MESH,
        )

    def arrived(i):
        x = place(i)
        core_copy(i).wait_recv()
        d1[x] = d0[my_c * nx + x] + rc[x]

    def step(i, carry):
        predict(other_c, place(i))
        core_copy(i).start()
        predict(my_c, place(i))

        @pl.when(i > 0)
        def _():
            arrived(i - 1)
            x_copy(i - 1).start()

        return carry

    lax.fori_loop(0, nx, step, 0)
    arrived(nx - 1)
    total = d1[my_x]
    for i in range(nx - 1):
        x_copy(i).wait()
        total = total + rx[i]
    d2[...] = total
    for i in range(nx):
        core_copy(i).wait_send()

    owning = my_y < owners
    copies = [
        push(
            d2.at[pl.ds(lax.rem((my_y + d) % ny, owners) * yt, yt)],
            ry.at[d - 1],
            (my_s, pts_at((my_y + d) % ny, my_z, my_xc)),
        )
        for d in range(1, ny)
    ]
    for d, copy in zip(range(1, ny), copies):
        pl.when((my_y + d) % ny < owners)(copy.start)
    for d, copy in zip(range(1, ny), copies):
        pl.when((my_y + d) % ny < owners)(copy.wait_send)
        pl.when(owning)(copy.wait_recv)

    first_tile = (my_c * nx + my_x) * xt
    held = lax.rem(my_y, owners)
    y_tile = first_tile + held * yt
    z_copies = [push(d3, rz.at[my_z], (my_s, pts_at(my_y, (my_z + d) % nz, my_xc))) for d in range(1, nz)]

    @pl.when(owning)
    def _():
        total = d2[pl.ds(held * yt, yt)]
        for d in range(1, ny):
            total = total + ry[d - 1]
        d3[...] = total
        finish(run(z_copies))
        rz[my_z] = d3[...]
        total = rz[0]
        for z in range(1, nz):
            total = total + rz[z]
        for i in range(yt):
            s = (y_tile + i) // rtiles
            live = lax.broadcasted_iota(jnp.int32, (1, steps), 1) < len_ref[s]
            weight = jnp.where(live, noise_ref[pl.ds(s, 1), :], 0.0) * cfg["scale_points"]
            value = dot_table(total[i] * weight, tab["dft"][0], tab["dft"][1])
            resb[y_tile + i] = value.astype(bf16)

    def piece(c, x, y):
        return resb.at[pl.ds((c * nx + x) * xt + lax.rem(y, owners) * yt, yt)]

    mine = piece(my_c, my_x, my_y)
    y_copies = [push(mine, mine, (my_s, pts_at((my_y + d) % ny, my_z, my_xc))) for d in range(1, ny)]
    for copy in y_copies:
        pl.when(owning)(copy.start)
    x_copies, c_copies = {}, {}
    for d in near_y:
        y = (my_y + ny - d) % ny
        if d:
            pl.when(y < owners)(y_copies[d - 1].wait_recv)
        here = piece(my_c, my_x, y)
        x_copies[d] = [
            push(here, here, (my_s, pts_at(my_y, my_z, ((my_x + e) % nx) * nc + my_c))) for e in range(1, nx)
        ]
        sources = [piece(my_c, (my_x + nx - e) % nx, y) for e in range(nx)]
        c_copies[d] = [push(source, source, (my_s, other)) for source in sources]
        pl.when(y < owners)(lambda d=d: run(x_copies[d] + c_copies[d][:1]) and None)
    for d in near_y:
        y = (my_y + ny - d) % ny

        @pl.when(y < owners)
        def _(d=d):
            for e in range(1, nx):
                x_copies[d][e - 1].wait_recv()
                c_copies[d][e].start()

    for copy in y_copies:
        pl.when(owning)(copy.wait_send)
    for d in near_y:
        y = (my_y + ny - d) % ny

        @pl.when(y < owners)
        def _(d=d):
            for copy in x_copies[d]:
                copy.wait_send()
            finish(c_copies[d])

    def widen(s, carry):
        for b in range(rtiles):
            rr = pl.ds(b * SUB, SUB)
            for j, span in enumerate(spans):
                c = resb[s * rtiles + b, :, span].astype(f32)
                d = resb[s * rtiles + b, :, pl.ds(steps + j * width, width)].astype(f32)
                q1[s, rr, span] = c
                q2[s, rr, span] = jnp.where(first_8, d, d - c) if j == 0 else d - c
                q3[s, rr, span] = c + d
        return carry

    lax.fori_loop(0, sensors, widen, 0)

    def contract_back(i, carry):
        for j, span in enumerate(spans):
            acc = {}
            for s in range(sensors):
                for u in range(2):
                    ka, kb, kc = (same_row(k, j, s, 2 * i + u) for k in (k4, k2, k3))
                    for b in range(rtiles):
                        rr = pl.ds(b * SUB, SUB)
                        term = (ka * q1[s, rr, span], kb * q2[s, rr, span], kc * q3[s, rr, span])
                        old = acc.get((u, b))
                        acc[u, b] = term if old is None else tuple(o + t for o, t in zip(old, term))
            for (u, b), (p1, p2, p3) in acc.items():
                combine((p1, p2, p1 + p3), j, adj, (2 * i + u, pl.ds(b * SUB, SUB)))
        return carry

    few = points // 2
    sends = []
    for h in range(2):
        lax.fori_loop(h * few // 2, (h + 1) * few // 2, contract_back, 0)
        value = adj[h * few : (h + 1) * few].reshape(few * rhs, 2 * steps)
        value = dot_table(value, tab["dft"][0], tab["dft"][1], BOTH_LAST)
        for j in range(len(spans)):
            gs[j, h * few * rhs : (h + 1) * few * rhs] = value[:, j * width : (j + 1) * width]
        for k in range(ns):
            parts = []
            for j in range(len(spans)):
                lines = [
                    gs[j, pl.ds(h * few * rhs + k * own_rhs + r, few, stride=rhs), :] for r in range(own_rhs)
                ]
                parts.append(jnp.concatenate(lines, axis=0))
            gk[h, k] = jnp.concatenate(parts, axis=1).astype(bf16)
        sends += run([push(gk.at[h, (my_s + d) % ns], rg.at[h, d - 1], ((my_s + d) % ns, me)) for d in range(1, ns)])
    finish(sends)
    sums = []
    for h in range(2):
        total = gk[h, my_s].astype(f32)
        for d in range(1, ns):
            total = total + rg[h, d - 1].astype(f32)
        sums.append(total)
    total = jnp.concatenate(
        [sums[h][r * few : (r + 1) * few] for r in range(own_rhs) for h in range(2)], axis=0
    )
    total = total * cfg["scale_sensors"]
    if rows < lane_pad:
        total = jnp.concatenate([total, jnp.zeros((lane_pad - rows, steps), f32)], axis=0)
    t1[...] = jnp.transpose(total).reshape(ny, nz, 2 * nxc, lane_pad).astype(bf16)

    copies = run(
        [
            push(t1.at[(my_y + d) % ny], u1.at[my_y], (my_s, pts_at((my_y + d) % ny, my_z, my_xc)))
            for d in range(1, ny)
        ]
    )
    u1[my_y] = t1[my_y]
    relay(copies, u1, u2)
    flat[...] = u2[...].astype(f32).reshape(nyz * 2 * nxc, lane_pad)
    for j in range(nxc):
        for e in range(2):
            s4[j, e] = flat[pl.ds(2 * j + e, nyz, stride=2 * nxc), :].astype(bf16)
    copies = run(
        [
            push(s4.at[(my_xc + d) % nxc], u3.at[my_xc], (my_s, pts_at(my_y, my_z, (my_xc + d) % nxc)))
            for d in range(1, nxc)
        ]
    )
    u3[my_xc] = s4[my_xc]
    finish(copies)

    modes = jnp.zeros((grid_rows, chunks * LANES), f32)
    for e in range(2):
        field = u3[:, e].reshape(npts, lane_pad)
        field = dot(tab["gather_rows"][0], field, RIGHT) + dot(tab["gather_rows"][1], field, RIGHT)
        for h in range(2):
            part = field[h * grid_rows : (h + 1) * grid_rows]
            modes = modes + dot_table(part, tab["in_half"][0, h, e], tab["in_half"][1, h, e])
    for g in range(chunks):
        z = modes_out(modes[:, g * LANES : (g + 1) * LANES])
        z = table_dot(tab["cxt"][0], tab["cxt"][1], z)
        z = dot_table(z, tab["cols_out"][0], tab["cols_out"][1])
        for i in range(per):
            out_ref[g * per + i] = z[:, i * GY : (i + 1) * GY]


def on_device(shape, params, kernel, coupled, noise_prec, obs_len):
    ny, nz, nx, nc = shape
    ns = lax.axis_size("sens")
    npts = lax.axis_size("pts")
    own_rhs, own_steps, total_points = params.shape
    sensors, points, steps = kernel.shape[1], kernel.shape[2], kernel.shape[3] - 1
    grid_rows = total_points // GY
    rhs = own_rhs * ns
    lane_pad = LANES
    tiles = sensors * rhs // SUB
    xt = tiles // (nc * nx)
    owners = max(k for k in range(1, ny + 1) if xt % k == 0)
    yt = xt // owners
    rows = own_rhs * points
    fields = own_rhs * own_steps
    assert xt % (2 * (rhs // SUB)) == 0
    assert own_steps == 2 and points == HALF and npts == ny * nz * nx * nc and rows <= lane_pad
    cfg = dict(
        shape=shape,
        sens=ns,
        sensors=sensors,
        points=points,
        steps=steps,
        own_rhs=own_rhs,
        lane_pad=lane_pad,
        grid_rows=grid_rows,
        owners=owners,
        scale_points=1.0 / math.sqrt(total_points),
        scale_sensors=1.0 / math.sqrt(sensors * ns),
    )
    tables = make_tables(grid_rows, shape, own_rhs, steps, lane_pad)
    tables = [jnp.asarray(tables[name]) for name in TABLES]
    field = params.reshape(fields, grid_rows, GY)
    nxc, nyz = nx * nc, ny * nz
    vm = pltpu.VMEM
    scratch = [vm(t.shape, t.dtype) for t in tables]
    scratch += [vm(kernel.shape, kernel.dtype)]
    scratch += [vm((steps // min(LANES, steps), sensors, points, min(LANES, steps)), f32)] * 4
    scratch += [vm((ny, nz, 2, nxc, lane_pad), f32)] * 2
    scratch += [vm((nz, ny, 2, nxc, lane_pad), f32)]
    scratch += [vm((nxc, 2, nyz, lane_pad), f32)] * 2
    scratch += [vm((ns, rows, 2 * steps), bf16), vm((2 * steps // min(LANES, steps), ns * rows, min(LANES, steps)), f32)]
    scratch += [vm((points, rhs, steps), f32)] * 3
    scratch += [vm((sensors, rhs, 2 * steps), f32)]
    scratch += [vm((nc * nx, xt, SUB, steps), f32)] + [vm((nx, xt, SUB, steps), f32)] * 2
    scratch += [vm((max(nx - 1, 1), xt, SUB, steps), f32), vm((xt, SUB, steps), f32)]
    scratch += [vm((max(ny - 1, 1), yt, SUB, steps), f32), vm((yt, SUB, steps), f32)]
    scratch += [vm((nz, yt, SUB, steps), f32)]
    scratch += [vm((tiles, SUB, 2 * steps), bf16)]
    scratch += [vm((sensors, rhs, steps), f32)] * 3
    scratch += [vm((points, rhs, 2 * steps), f32), vm((steps // min(LANES, steps), points * rhs, min(LANES, steps)), f32)]
    scratch += [vm((2, ns, rows // 2, steps), bf16), vm((2, max(ns - 1, 1), rows // 2, steps), bf16)]
    scratch += [vm((ny, nz, 2 * nxc, lane_pad), bf16)] * 2 + [vm((nz, ny, 2 * nxc, lane_pad), bf16)]
    scratch += [vm((nxc, 2, nyz, lane_pad), bf16)] * 2
    scratch += [vm((nyz * 2 * nxc, lane_pad), f32)]
    copies = 4 * ny + 2 * ny * nz + 2 * nxc + 3 * ns + 4 * nx + 2 * ny * nx + nz
    scratch += [
        pltpu.SemaphoreType.DMA((len(tables) + 1,)),
        pltpu.SemaphoreType.DMA((copies,)),
        pltpu.SemaphoreType.DMA((copies,)),
    ]
    whole = pl.BlockSpec(memory_space=pltpu.VMEM)
    scalars = pl.BlockSpec(memory_space=pltpu.SMEM)
    anywhere = pl.BlockSpec(memory_space=pl.ANY)
    out = pl.pallas_call(
        lambda *refs: kernel_body(cfg, *refs),
        out_shape=jax.ShapeDtypeStruct((fields, grid_rows, GY), f32),
        in_specs=[whole, anywhere, whole, whole, scalars] + [anywhere] * len(tables),
        out_specs=whole,
        scratch_shapes=scratch,
        compiler_params=pltpu.CompilerParams(
            collective_id=0, has_side_effects=True, vmem_limit_bytes=60 * 1024 * 1024
        ),
        name="hessian_action",
    )(field, kernel, coupled.T, noise_prec, obs_len, *tables)
    return out.reshape(params.shape)


def solution(mesh, shape=PTS_SHAPE):
    placed = (
        P("sens", "pts", None),
        P(None, "sens", "pts", None),
        P("sens", "pts"),
        P("sens", None),
        P("sens"),
    )
    return jax.shard_map(
        lambda *args: on_device(shape, *args),
        mesh=mesh,
        in_specs=placed,
        out_specs=P("sens", "pts", None),
        check_vma=False,
    )
```

```python
import functools
import math

import jax
import jax.numpy as jnp
import numpy as np
from jax import lax
from jax.experimental import pallas as pl
from jax.experimental.pallas import tpu as pltpu
from jax.sharding import PartitionSpec as P

GY = 32
HALF = GY // 2
LANES = 128
SUB = 8
prior_delta = 0.5
prior_gamma = 1.0
f32 = jnp.float32
bf16 = jnp.bfloat16
PTS_SHAPE = (8, 2, 4, 2)


def cosine_table(count):
    k = np.arange(count)[:, None]
    i = np.arange(count)[None, :]
    norm = np.where(k == 0, math.sqrt(1.0 / count), math.sqrt(2.0 / count))
    return np.cos(math.pi * k * (2 * i + 1) / (2 * count)) * norm


def prior_symbol(rows, cols):
    er = 2.0 - 2.0 * np.cos(math.pi * np.arange(rows) / rows)
    ec = 2.0 - 2.0 * np.cos(math.pi * np.arange(cols) / cols)
    return 1.0 / (prior_delta + prior_gamma * (er[:, None] + ec[None, :]))


def packed_dft(steps):
    t = np.arange(steps)[:, None]
    f = np.arange(steps)[None, :]
    angle = 2.0 * math.pi * ((t * f) % (2 * steps)) / (2 * steps)
    real, imag = np.cos(angle), -np.sin(angle)
    imag[:, 0] = np.cos(math.pi * t[:, 0])
    return np.concatenate([real, imag], axis=1) / math.sqrt(2 * steps)


def split_table(table):
    high = table.astype(np.float32).astype(bf16)
    low = (table - high.astype(np.float64)).astype(np.float32).astype(bf16)
    return np.stack([high, low])


def make_tables(grid_rows, shape, own_rhs, steps, lane_pad):
    ny, nz, nx, nc = shape
    nxc = nx * nc
    npts = ny * nz * nxc
    cx, cy = cosine_table(grid_rows), cosine_table(GY)
    fields = 2 * own_rhs
    per = LANES // GY
    cols_in = np.kron(np.eye(per), cy.T)
    cols_out = np.kron(np.eye(per), cy)
    spread_rows = np.repeat(cx.T, 2, axis=0)
    out_half = np.zeros((2, fields * GY, 2 * lane_pad))
    in_half = np.zeros((2, 2, lane_pad, fields * GY))
    for h in range(2):
        part = cy[:, h * HALF : (h + 1) * HALF]
        for r in range(own_rhs):
            for e in range(2):
                field = (2 * r + e) * GY
                lane = r * HALF
                out_half[h, field : field + GY, e * lane_pad + lane : e * lane_pad + lane + HALF] = part
                in_half[h, e, lane : lane + HALF, field : field + GY] = part.T
    row = np.arange(npts)
    xc, rest = row // (nz * ny), row % (nz * ny)
    z, y = rest // ny, rest % ny
    owner = (y * nz + z) * nxc + xc
    gather_rows = np.zeros((2 * grid_rows, npts))
    for h in range(2):
        gather_rows[h * grid_rows : (h + 1) * grid_rows] = cx[:, owner // 2] * (owner % 2 == h)[None, :]
    dft = packed_dft(steps)
    dft_pairs = np.stack([dft[2 * owner], dft[2 * owner + 1]])
    small = dict(cols_in=cols_in, cols_out=cols_out, cx=cx, cxt=cx.T, spread_rows=spread_rows)
    small.update(out_half=out_half, gather_rows=gather_rows, in_half=in_half, dft=dft, dft_pairs=dft_pairs)
    tables = {name: split_table(table) for name, table in small.items()}
    tables["sigma"] = np.tile(prior_symbol(grid_rows, GY), (1, per)).astype(np.float32)
    return tables


TABLES = ("cols_in", "cx", "sigma", "spread_rows", "out_half")
FIRST = len(TABLES)
TABLES += ("dft_pairs", "dft", "gather_rows", "in_half")
TABLES += ("cols_out", "cxt")

RIGHT = ((1,), (0,))
BOTH_LAST = ((1,), (1,))
BOTH_FIRST = ((0,), (0,))


def dot(a, b, dims):
    return lax.dot_general(a, b, (dims, ((), ())), preferred_element_type=f32)


def halves(v):
    high = v.astype(bf16)
    return high, (v - high.astype(f32)).astype(bf16)


def dot_table(v, high, low, dims=RIGHT):
    vh, vl = halves(v)
    return dot(vh, high, dims) + (dot(vl, high, dims) + dot(vh, low, dims))


def same_row(ref, j, s, p):
    return jnp.broadcast_to(ref[j, s, pl.ds(p, 1), :], (SUB, ref.shape[-1]))


def table_dot(high, low, v):
    vh, vl = halves(v)
    return dot(high, vh, RIGHT) + (dot(high, vl, RIGHT) + dot(low, vh, RIGHT))


def kernel_body(cfg, *refs):
    (ny, nz, nx, nc), ns = cfg["shape"], cfg["sens"]
    nxc, nyz = nx * nc, ny * nz
    npts = nyz * nxc
    sensors, points, steps, own_rhs = cfg["sensors"], cfg["points"], cfg["steps"], cfg["own_rhs"]
    rhs = own_rhs * ns
    lane_pad = cfg["lane_pad"]
    grid_rows = cfg["grid_rows"]
    tiles = sensors * rhs // SUB
    rtiles = rhs // SUB
    xt = tiles // (nc * nx)
    owners = cfg["owners"]
    yt = xt // owners
    chunks = 2 * own_rhs * GY // LANES
    rows = own_rhs * points
    per = LANES // GY
    width = min(LANES, steps)

    field_ref, kernel_hbm, mask_ref, noise_ref, len_ref = refs[:5]
    ntab = len(TABLES)
    table_hbm = refs[5 : 5 + ntab]
    out_ref = refs[5 + ntab]
    scratch = list(refs[6 + ntab :])
    table_vmem = scratch[:ntab]
    (kraw, k1, k2, k3, k4, s1, r1, r2, s3, r3, sp, xf, x1, x2, x3, obs, d0, rc, d1, rx, d2, ry, d3, rz) = scratch[
        ntab : ntab + 24
    ]
    (resb, q1, q2, q3, adj, gs, gk, rg, t1, u1, u2, s4, u3, flat, load_sem, send_sem, recv_sem) = scratch[ntab + 24 :]
    tab = dict(zip(TABLES, table_vmem))

    my_s = lax.axis_index("sens")
    me = lax.axis_index("pts")
    my_y = me // (nz * nxc)
    my_z = (me // nxc) % nz
    my_xc = me % nxc
    my_x = my_xc // nc
    my_c = my_xc % nc

    def pts_at(y, z, xc):
        return (y * nz + z) * nxc + xc

    loads = [pltpu.make_async_copy(a, b, load_sem.at[i]) for i, (a, b) in enumerate(zip(table_hbm, table_vmem))]
    loads.append(pltpu.make_async_copy(kernel_hbm, kraw, load_sem.at[ntab]))
    for copy in loads:
        copy.start()

    partners = [(my_s, pts_at((my_y + d) % ny, my_z, my_xc)) for d in range(1, ny)]
    partners += [(my_s, pts_at(my_y, (my_z + d) % nz, my_xc)) for d in range(1, nz)]
    partners += [(my_s, pts_at(my_y, my_z, (my_xc + d) % nxc)) for d in range(1, nxc)]
    partners += [((my_s + d) % ns, me) for d in range(1, ns)]
    barrier = pltpu.get_barrier_semaphore()
    for target in partners:
        pl.semaphore_signal(barrier, inc=1, device_id=target, device_id_type=pl.DeviceIdType.MESH)

    used = [0]

    spans = [pl.ds(j * width, width) for j in range(steps // width)]

    def push(src, dst, target):
        i = used[0]
        used[0] += 1
        return pltpu.make_async_remote_copy(
            src_ref=src,
            dst_ref=dst,
            send_sem=send_sem.at[i],
            recv_sem=recv_sem.at[i],
            device_id=target,
            device_id_type=pl.DeviceIdType.MESH,
        )

    def run(copies):
        for copy in copies:
            copy.start()
        return copies

    def finish(copies):
        for copy in copies:
            copy.wait()

    near_y = sorted(range(ny), key=lambda d: min(d, ny - d))

    def relay(copies, came, left):
        onward = []
        for d in near_y:
            y = (my_y + ny - d) % ny
            if d:
                copies[d - 1].wait_recv()
            for e in range(1, nz):
                z = (my_z + e) % nz
                onward += run([push(came.at[y, z], left.at[my_z, y], (my_s, pts_at(my_y, z, my_xc)))])
        left[my_z] = came[:, my_z]
        for copy in copies:
            copy.wait_send()
        finish(onward)

    def modes_out(z):
        return z * tab["sigma"][...]

    for copy in loads[:FIRST]:
        copy.wait()
    parity = lax.broadcasted_iota(jnp.int32, (npts, 2 * lane_pad), 0) % 2
    filtered = [jnp.zeros((npts, 2 * lane_pad), f32)] * 2
    for g in range(chunks):
        z = jnp.zeros((grid_rows, LANES), f32)
        for i in range(per):
            lines = pl.ds(i * GY, GY)
            z = z + dot_table(field_ref[g * per + i], tab["cols_in"][0, lines, :], tab["cols_in"][1, lines, :])
        z = modes_out(table_dot(tab["cx"][0], tab["cx"][1], z))
        z = table_dot(tab["spread_rows"][0], tab["spread_rows"][1], z)
        for h in range(2):
            span = pl.ds(g * LANES, LANES)
            filtered[h] = filtered[h] + dot_table(z, tab["out_half"][0, h, span, :], tab["out_half"][1, h, span, :])
    mixed = jnp.where(parity == 0, filtered[0], filtered[1])
    for e in range(2):
        s1[:, :, e] = mixed[:, e * lane_pad : (e + 1) * lane_pad].reshape(ny, nz, nxc, lane_pad)

    pl.semaphore_wait(barrier, len(partners))
    copies = run(
        [
            push(s1.at[(my_y + d) % ny], r1.at[my_y], (my_s, pts_at((my_y + d) % ny, my_z, my_xc)))
            for d in range(1, ny)
        ]
    )
    r1[my_y] = s1[my_y]

    for copy in loads[FIRST:]:
        copy.wait()
    first16 = lax.broadcasted_iota(jnp.int32, (points, steps), 1) == 0

    for s in range(sensors):
        keep = mask_ref[:, s : s + 1].astype(f32)
        real = kraw[0, s, :, :steps].astype(f32)
        imag = kraw[1, s, :, :steps].astype(f32)
        last = kraw[0, s, :, steps : steps + 1].astype(f32)
        imag = jnp.where(first16, 0.0, imag)
        plain = jnp.where(first16, last, real)
        for ref, value in ((k1, real + imag), (k2, plain), (k3, imag), (k4, real - imag)):
            for j, span in enumerate(spans):
                ref[j, s] = (value * keep)[:, j * width : (j + 1) * width]

    relay(copies, r1, r2)
    flat[...] = r2[...].reshape(nyz * 2 * nxc, lane_pad)
    for j in range(nxc):
        for e in range(2):
            s3[j, e] = flat[pl.ds(e * nxc + j, nyz, stride=2 * nxc), :]
    copies = run(
        [
            push(s3.at[(my_xc + d) % nxc], r3.at[my_xc], (my_s, pts_at(my_y, my_z, (my_xc + d) % nxc)))
            for d in range(1, nxc)
        ]
    )
    r3[my_xc] = s3[my_xc]
    finish(copies)

    spectra = jnp.zeros((lane_pad, 2 * steps), f32)
    for e in range(2):
        series = r3[:, e].reshape(npts, lane_pad)
        spectra = spectra + dot_table(series, tab["dft_pairs"][0, e], tab["dft_pairs"][1, e], BOTH_FIRST)
    first_r = lax.broadcasted_iota(jnp.int32, (rhs, width), 1) == 0
    first_8 = lax.broadcasted_iota(jnp.int32, (SUB, width), 1) == 0
    def combine(real_terms, j, out, at):
        p1, p2, real = real_terms
        imag = p1 + p2
        if j == 0:
            out[at + (pl.ds(0, width),)] = jnp.where(first_8, real, real + real)
            out[at + (pl.ds(steps, width),)] = jnp.where(first_8, p2, imag + imag)
        else:
            out[at + (spans[j],)] = real + real
            out[at + (pl.ds(steps + j * width, width),)] = imag + imag

    def contract(j, i, carry):
        span, acc = spans[j], {}
        for p in range(points):
            for u in range(2):
                ka, kb, kc = (same_row(k, j, 2 * i + u, p) for k in (k1, k2, k3))
                for b in range(rtiles):
                    rr = pl.ds(b * SUB, SUB)
                    term = (ka * x1[p, rr, span], kb * x2[p, rr, span], kc * x3[p, rr, span])
                    old = acc.get((u, b))
                    acc[u, b] = term if old is None else tuple(o + t for o, t in zip(old, term))
        for (u, b), (p1, p2, p3) in acc.items():
            combine((p1, p2, p1 - p3), j, obs, (2 * i + u, pl.ds(b * SUB, SUB)))
        return carry

    parts = len(spans)
    sends = []
    for j in range(parts):
        sp[j, my_s] = jnp.concatenate(
            [
                spectra[:rows, j * width : (j + 1) * width],
                spectra[:rows, steps + j * width : steps + (j + 1) * width],
            ],
            axis=1,
        ).astype(bf16)
        sends.append(
            run([push(sp.at[j, my_s], sp.at[j, my_s], ((my_s + d) % ns, me)) for d in range(1, ns)])
        )
    for j, span in enumerate(spans):
        finish(sends[j])
        for k in range(ns):
            xf[j, k * rows : (k + 1) * rows] = sp[j, k, :, :width].astype(f32)
            xf[parts + j, k * rows : (k + 1) * rows] = sp[j, k, :, width:].astype(f32)
        for p in range(points):
            c = xf[j, pl.ds(p, rhs, stride=points), :]
            d = xf[parts + j, pl.ds(p, rhs, stride=points), :]
            x1[p, :, span] = c
            x2[p, :, span] = jnp.where(first_r, d, d - c) if j == 0 else d - c
            x3[p, :, span] = c + d
        if j < parts - 1:
            lax.fori_loop(0, sensors // 2, functools.partial(contract, j), 0)

    block = xt // rtiles

    def predict(c, x):
        first = (c * nx + x) * block
        lax.fori_loop(first // 2, (first + block) // 2, functools.partial(contract, parts - 1), 0)
        value = obs[pl.ds(first, block)].reshape(block * rhs, 2 * steps)
        value = dot_table(value, tab["dft"][0], tab["dft"][1], BOTH_LAST)
        d0[c * nx + x] = value.reshape(xt, SUB, steps)

    other_c = (my_c + 1) % nc
    other = pts_at(my_y, my_z, my_x * nc + other_c)
    base_c, base_x = used[0], used[0] + nx
    used[0] += 2 * nx

    def place(i):
        return (my_x + i + 1) % nx

    def core_copy(i):
        x = place(i)
        return pltpu.make_async_remote_copy(
            src_ref=d0.at[other_c * nx + x],
            dst_ref=rc.at[x],
            send_sem=send_sem.at[base_c + i],
            recv_sem=recv_sem.at[base_c + i],
            device_id=(my_s, other),
            device_id_type=pl.DeviceIdType.MESH,
        )

    def x_copy(i):
        x = place(i)
        return pltpu.make_async_remote_copy(
            src_ref=d1.at[x],
            dst_ref=rx.at[i],
            send_sem=send_sem.at[base_x + i],
            recv_sem=recv_sem.at[base_x + i],
            device_id=(my_s, pts_at(my_y, my_z, x * nc + my_c)),
            device_id_type=pl.DeviceIdType.MESH,
        )

    def arrived(i):
        x = place(i)
        core_copy(i).wait_recv()
        d1[x] = d0[my_c * nx + x] + rc[x]

    def step(i, carry):
        predict(other_c, place(i))
        core_copy(i).start()
        predict(my_c, place(i))

        @pl.when(i > 0)
        def _():
            arrived(i - 1)
            x_copy(i - 1).start()

        return carry

    lax.fori_loop(0, nx, step, 0)
    arrived(nx - 1)
    total = d1[my_x]
    for i in range(nx - 1):
        x_copy(i).wait()
        total = total + rx[i]
    d2[...] = total
    for i in range(nx):
        core_copy(i).wait_send()

    owning = my_y < owners
    copies = [
        push(
            d2.at[pl.ds(lax.rem((my_y + d) % ny, owners) * yt, yt)],
            ry.at[d - 1],
            (my_s, pts_at((my_y + d) % ny, my_z, my_xc)),
        )
        for d in range(1, ny)
    ]
    for d, copy in zip(range(1, ny), copies):
        pl.when((my_y + d) % ny < owners)(copy.start)
    for d, copy in zip(range(1, ny), copies):
        pl.when((my_y + d) % ny < owners)(copy.wait_send)
        pl.when(owning)(copy.wait_recv)

    first_tile = (my_c * nx + my_x) * xt
    held = lax.rem(my_y, owners)
    y_tile = first_tile + held * yt
    z_copies = [push(d3, rz.at[my_z], (my_s, pts_at(my_y, (my_z + d) % nz, my_xc))) for d in range(1, nz)]

    @pl.when(owning)
    def _():
        total = d2[pl.ds(held * yt, yt)]
        for d in range(1, ny):
            total = total + ry[d - 1]
        d3[...] = total
        finish(run(z_copies))
        rz[my_z] = d3[...]
        total = rz[0]
        for z in range(1, nz):
            total = total + rz[z]
        for i in range(yt):
            s = (y_tile + i) // rtiles
            live = lax.broadcasted_iota(jnp.int32, (1, steps), 1) < len_ref[s]
            weight = jnp.where(live, noise_ref[pl.ds(s, 1), :], 0.0) * cfg["scale_points"]
            value = dot_table(total[i] * weight, tab["dft"][0], tab["dft"][1])
            resb[y_tile + i] = value.astype(bf16)

    def piece(c, x, y):
        return resb.at[pl.ds((c * nx + x) * xt + lax.rem(y, owners) * yt, yt)]

    mine = piece(my_c, my_x, my_y)
    y_copies = [push(mine, mine, (my_s, pts_at((my_y + d) % ny, my_z, my_xc))) for d in range(1, ny)]
    for copy in y_copies:
        pl.when(owning)(copy.start)
    x_copies, c_copies = {}, {}
    for d in near_y:
        y = (my_y + ny - d) % ny
        if d:
            pl.when(y < owners)(y_copies[d - 1].wait_recv)
        here = piece(my_c, my_x, y)
        x_copies[d] = [
            push(here, here, (my_s, pts_at(my_y, my_z, ((my_x + e) % nx) * nc + my_c))) for e in range(1, nx)
        ]
        sources = [piece(my_c, (my_x + nx - e) % nx, y) for e in range(nx)]
        c_copies[d] = [push(source, source, (my_s, other)) for source in sources]
        pl.when(y < owners)(lambda d=d: run(x_copies[d] + c_copies[d][:1]) and None)
    for d in near_y:
        y = (my_y + ny - d) % ny

        @pl.when(y < owners)
        def _(d=d):
            for e in range(1, nx):
                x_copies[d][e - 1].wait_recv()
                c_copies[d][e].start()

    for copy in y_copies:
        pl.when(owning)(copy.wait_send)
    for d in near_y:
        y = (my_y + ny - d) % ny

        @pl.when(y < owners)
        def _(d=d):
            for copy in x_copies[d]:
                copy.wait_send()
            finish(c_copies[d])

    def widen(s, carry):
        for b in range(rtiles):
            rr = pl.ds(b * SUB, SUB)
            for j, span in enumerate(spans):
                c = resb[s * rtiles + b, :, span].astype(f32)
                d = resb[s * rtiles + b, :, pl.ds(steps + j * width, width)].astype(f32)
                q1[s, rr, span] = c
                q2[s, rr, span] = jnp.where(first_8, d, d - c) if j == 0 else d - c
                q3[s, rr, span] = c + d
        return carry

    lax.fori_loop(0, sensors, widen, 0)

    def contract_back(i, carry):
        for j, span in enumerate(spans):
            acc = {}
            for s in range(sensors):
                for u in range(2):
                    ka, kb, kc = (same_row(k, j, s, 2 * i + u) for k in (k4, k2, k3))
                    for b in range(rtiles):
                        rr = pl.ds(b * SUB, SUB)
                        term = (ka * q1[s, rr, span], kb * q2[s, rr, span], kc * q3[s, rr, span])
                        old = acc.get((u, b))
                        acc[u, b] = term if old is None else tuple(o + t for o, t in zip(old, term))
            for (u, b), (p1, p2, p3) in acc.items():
                combine((p1, p2, p1 + p3), j, adj, (2 * i + u, pl.ds(b * SUB, SUB)))
        return carry

    few = points // 2
    sends = []
    for h in range(2):
        lax.fori_loop(h * few // 2, (h + 1) * few // 2, contract_back, 0)
        value = adj[h * few : (h + 1) * few].reshape(few * rhs, 2 * steps)
        value = dot_table(value, tab["dft"][0], tab["dft"][1], BOTH_LAST)
        for j in range(len(spans)):
            gs[j, h * few * rhs : (h + 1) * few * rhs] = value[:, j * width : (j + 1) * width]
        for k in range(ns):
            pieces = []
            for j in range(len(spans)):
                lines = [
                    gs[j, pl.ds(h * few * rhs + k * own_rhs + r, few, stride=rhs), :] for r in range(own_rhs)
                ]
                pieces.append(jnp.concatenate(lines, axis=0))
            gk[h, k] = jnp.concatenate(pieces, axis=1).astype(bf16)
        sends += run([push(gk.at[h, (my_s + d) % ns], rg.at[h, d - 1], ((my_s + d) % ns, me)) for d in range(1, ns)])
    finish(sends)
    sums = []
    for h in range(2):
        total = gk[h, my_s].astype(f32)
        for d in range(1, ns):
            total = total + rg[h, d - 1].astype(f32)
        sums.append(total)
    total = jnp.concatenate(
        [sums[h][r * few : (r + 1) * few] for r in range(own_rhs) for h in range(2)], axis=0
    )
    total = total * cfg["scale_sensors"]
    if rows < lane_pad:
        total = jnp.concatenate([total, jnp.zeros((lane_pad - rows, steps), f32)], axis=0)
    t1[...] = jnp.transpose(total).reshape(ny, nz, 2 * nxc, lane_pad).astype(bf16)

    copies = run(
        [
            push(t1.at[(my_y + d) % ny], u1.at[my_y], (my_s, pts_at((my_y + d) % ny, my_z, my_xc)))
            for d in range(1, ny)
        ]
    )
    u1[my_y] = t1[my_y]
    relay(copies, u1, u2)
    flat[...] = u2[...].astype(f32).reshape(nyz * 2 * nxc, lane_pad)
    for j in range(nxc):
        for e in range(2):
            s4[j, e] = flat[pl.ds(2 * j + e, nyz, stride=2 * nxc), :].astype(bf16)
    copies = run(
        [
            push(s4.at[(my_xc + d) % nxc], u3.at[my_xc], (my_s, pts_at(my_y, my_z, (my_xc + d) % nxc)))
            for d in range(1, nxc)
        ]
    )
    u3[my_xc] = s4[my_xc]
    finish(copies)

    modes = jnp.zeros((grid_rows, chunks * LANES), f32)
    for e in range(2):
        field = u3[:, e].reshape(npts, lane_pad)
        field = dot(tab["gather_rows"][0], field, RIGHT) + dot(tab["gather_rows"][1], field, RIGHT)
        for h in range(2):
            part = field[h * grid_rows : (h + 1) * grid_rows]
            modes = modes + dot_table(part, tab["in_half"][0, h, e], tab["in_half"][1, h, e])
    for g in range(chunks):
        z = modes_out(modes[:, g * LANES : (g + 1) * LANES])
        z = table_dot(tab["cxt"][0], tab["cxt"][1], z)
        z = dot_table(z, tab["cols_out"][0], tab["cols_out"][1])
        for i in range(per):
            out_ref[g * per + i] = z[:, i * GY : (i + 1) * GY]


def on_device(shape, params, kernel, coupled, noise_prec, obs_len):
    ny, nz, nx, nc = shape
    ns = lax.axis_size("sens")
    npts = lax.axis_size("pts")
    own_rhs, own_steps, total_points = params.shape
    sensors, points, steps = kernel.shape[1], kernel.shape[2], kernel.shape[3] - 1
    grid_rows = total_points // GY
    rhs = own_rhs * ns
    lane_pad = LANES
    tiles = sensors * rhs // SUB
    xt = tiles // (nc * nx)
    owners = max(k for k in range(1, ny + 1) if xt % k == 0)
    yt = xt // owners
    rows = own_rhs * points
    fields = own_rhs * own_steps
    assert xt % (2 * (rhs // SUB)) == 0
    assert own_steps == 2 and points == HALF and npts == ny * nz * nx * nc and rows <= lane_pad
    cfg = dict(
        shape=shape,
        sens=ns,
        sensors=sensors,
        points=points,
        steps=steps,
        own_rhs=own_rhs,
        lane_pad=lane_pad,
        grid_rows=grid_rows,
        owners=owners,
        scale_points=1.0 / math.sqrt(total_points),
        scale_sensors=1.0 / math.sqrt(sensors * ns),
    )
    tables = make_tables(grid_rows, shape, own_rhs, steps, lane_pad)
    tables = [jnp.asarray(tables[name]) for name in TABLES]
    field = params.reshape(fields, grid_rows, GY)
    nxc, nyz = nx * nc, ny * nz
    vm = pltpu.VMEM
    scratch = [vm(t.shape, t.dtype) for t in tables]
    scratch += [vm(kernel.shape, kernel.dtype)]
    scratch += [vm((steps // min(LANES, steps), sensors, points, min(LANES, steps)), f32)] * 4
    scratch += [vm((ny, nz, 2, nxc, lane_pad), f32)] * 2
    scratch += [vm((nz, ny, 2, nxc, lane_pad), f32)]
    scratch += [vm((nxc, 2, nyz, lane_pad), f32)] * 2
    scratch += [vm((steps // min(LANES, steps), ns, rows, 2 * min(LANES, steps)), bf16), vm((2 * steps // min(LANES, steps), ns * rows, min(LANES, steps)), f32)]
    scratch += [vm((points, rhs, steps), f32)] * 3
    scratch += [vm((sensors, rhs, 2 * steps), f32)]
    scratch += [vm((nc * nx, xt, SUB, steps), f32)] + [vm((nx, xt, SUB, steps), f32)] * 2
    scratch += [vm((max(nx - 1, 1), xt, SUB, steps), f32), vm((xt, SUB, steps), f32)]
    scratch += [vm((max(ny - 1, 1), yt, SUB, steps), f32), vm((yt, SUB, steps), f32)]
    scratch += [vm((nz, yt, SUB, steps), f32)]
    scratch += [vm((tiles, SUB, 2 * steps), bf16)]
    scratch += [vm((sensors, rhs, steps), f32)] * 3
    scratch += [vm((points, rhs, 2 * steps), f32), vm((steps // min(LANES, steps), points * rhs, min(LANES, steps)), f32)]
    scratch += [vm((2, ns, rows // 2, steps), bf16), vm((2, max(ns - 1, 1), rows // 2, steps), bf16)]
    scratch += [vm((ny, nz, 2 * nxc, lane_pad), bf16)] * 2 + [vm((nz, ny, 2 * nxc, lane_pad), bf16)]
    scratch += [vm((nxc, 2, nyz, lane_pad), bf16)] * 2
    scratch += [vm((nyz * 2 * nxc, lane_pad), f32)]
    copies = 4 * ny + 2 * ny * nz + 2 * nxc + 4 * ns + 4 * nx + 2 * ny * nx + nz
    scratch += [
        pltpu.SemaphoreType.DMA((len(tables) + 1,)),
        pltpu.SemaphoreType.DMA((copies,)),
        pltpu.SemaphoreType.DMA((copies,)),
    ]
    whole = pl.BlockSpec(memory_space=pltpu.VMEM)
    scalars = pl.BlockSpec(memory_space=pltpu.SMEM)
    anywhere = pl.BlockSpec(memory_space=pl.ANY)
    out = pl.pallas_call(
        lambda *refs: kernel_body(cfg, *refs),
        out_shape=jax.ShapeDtypeStruct((fields, grid_rows, GY), f32),
        in_specs=[whole, anywhere, whole, whole, scalars] + [anywhere] * len(tables),
        out_specs=whole,
        scratch_shapes=scratch,
        compiler_params=pltpu.CompilerParams(
            collective_id=0, has_side_effects=True, vmem_limit_bytes=60 * 1024 * 1024
        ),
        name="hessian_action",
    )(field, kernel, coupled.T, noise_prec, obs_len, *tables)
    return out.reshape(params.shape)


def solution(mesh, shape=PTS_SHAPE):
    placed = (
        P("sens", "pts", None),
        P(None, "sens", "pts", None),
        P("sens", "pts"),
        P("sens", None),
        P("sens"),
    )
    return jax.shard_map(
        lambda *args: on_device(shape, *args),
        mesh=mesh,
        in_specs=placed,
        out_specs=P("sens", "pts", None),
        check_vma=False,
    )
```
